512 devices in a mesh: rep: 4 (over y), own: 128 (over x, z, core).
Axes of the slice: x: 4, y: 4, z: 16, core: 2. Of those that a mesh axis runs over, the one named last changes fastest.
Arguments:
- owners: int32 [256, 1], replicated, may hold values from 0 to 127; in each aligned block of 256 rows (0 to 255, 256 to 511, ...) at most 4 rows name the same one
- inner_dense: float32 [4, 256, 65536], P('rep', None, 'own'), may hold values from -6 to 6
- anchor_dense: float32 [256, 65536], P(None, 'own'), may hold values from -6 to 6
- momentum_dense: float32 [512, 65536], P('own'), may hold values from -6 to 6
- inner_emb: float32 [4, 25600, 1024], P('rep', 'own'), may hold values from -6 to 6
- anchor_emb: float32 [25600, 1024], P('own'), may hold values from -6 to 6
- momentum_emb: float32 [25600, 64], P('own'), may hold values from -6 to 6
- basis: float32 [1024, 64], replicated, may hold values from -0.1875 to 0.1875
Outputs:
- new_dense: float32 [256, 65536], P(None, 'own')
- new_momentum_dense: float32 [512, 65536], P('own')
- new_emb: float32 [25600, 1024], P('own')
- new_momentum_emb: float32 [25600, 64], P('own')
The draws below stay inside these ranges and needn't reach their ends.
Inputs may be any that keep to these rules, and one draw needn't show every extreme that they name: `owners`: each owner position owns at most 4 blocks, and some position owns exactly 4.
All inputs are finite; a program needn't handle non-finite values.
Results may differ from the reference program's by a relative error of at most 0.00011.
Values sent between devices are 32-bit elements; how exact they have to be, the bound alone decides.
A program may use at most 64 MiB of HBM per device.

```python
import math
import jax
import jax.numpy as jnp
import numpy as np
from jax import lax

D = 1024
UR = 64
RANK = 64
NUNITS = 256
SLOTS = 4
VOCAB = 25600
GROUPS = 4
N_OWN = 128


def levels(own_key, shape, shards, smallest, high):
    factor_of = 1.0
    for axis_at, parts in shards:
        steps = jax.random.uniform(jax.random.fold_in(jax.random.fold_in(own_key, 6), axis_at), (parts,), jnp.float32, smallest / len(shards), high / len(shards))
        factor_of = factor_of * jnp.repeat(jnp.exp(steps), shape[axis_at] // parts).reshape((-1,) + (1,) * (len(shape) - 1 - axis_at))
    return factor_of


def shared_out(stream_key, own, number, rows, number_of, top, most, slope):
    order = jax.random.permutation(stream_key, number_of)
    heavy_load, ordinary = load_shares(number_of, rows * top, most, slope, True), load_shares(number_of, rows * top, most, slope, False)
    places = jnp.arange(number_of)

    def named(tallies, rotation):
        used = int((tallies > 0).sum())
        fixed = max(1, used // 4)
        moved = fixed + (places - fixed + rotation * (used - fixed)) % max(1, number_of - fixed)
        return jnp.zeros((number_of,), jnp.int32).at[order[jnp.where(places < fixed, places, moved)]].set(jnp.asarray(tallies, jnp.int32))

    tallies = jnp.where(number % 4 == 0, named(heavy_load, number // 4), named(ordinary, number - number // 4 - 1))
    mixed = jax.random.permutation(jax.random.fold_in(own, 3), number_of)
    donor, sink = mixed[0:number_of // 2 * 2:2], mixed[1:number_of // 2 * 2:2]
    slack = jnp.minimum(tallies[donor] - 1, most - tallies[sink]) // 2
    slack = jnp.where((donor == order[0]) | (sink == order[0]) | (tallies[sink] == 0), 0, jnp.maximum(slack, 0))
    moved = jax.random.randint(jax.random.fold_in(own, 4), (number_of // 2,), 0, 1 << 20) % (slack + 1)
    tallies = tallies.at[donor].add(-moved).at[sink].add(moved)
    labels = jnp.searchsorted(jnp.cumsum(tallies), jnp.arange(rows * top), side="right").astype(jnp.int32)
    grid = labels.reshape(top, rows).T
    grid = grid[jax.random.permutation(jax.random.fold_in(own, 1), rows)]
    rotation = jax.random.randint(jax.random.fold_in(own, 2), (rows, 1), 0, top)
    return jnp.take_along_axis(grid, (jnp.arange(top)[None, :] + rotation) % top, axis=1)


def load_shares(amount, total, bound, skew, full):
    weights = [(1 << 20) // math.isqrt(grade ** skew) + 1 for grade in range(1, amount + 1)]
    largest = bound if full else min(bound, max(-(-total // amount), total * weights[0] // sum(weights)))
    least = 1 if total - largest >= amount - 1 else 0
    holding, surplus = [largest] + [least] * (amount - 1), total - largest - least * (amount - 1)
    while surplus > 0:
        movable = [i for i in range(1, amount) if holding[i] < largest] or [i for i in range(1, amount) if holding[i] < bound]
        whole, left = sum([weights[i] for i in movable]), surplus
        for i in movable:
            addition = min(bound - holding[i], max(1, left * weights[i] // whole), surplus)
            holding[i] = holding[i] + addition
            surplus = surplus - addition
    return np.array(holding)


def bell_draw(rng, extent, width, most, cuts=(), held_as=jnp.bfloat16):
    values = width * jax.random.normal(rng, extent, jnp.float32)
    if cuts:
        values = values * levels(rng, extent, cuts, -0.22, 0.18)
    return jnp.clip(values, -most, most).astype(held_as)


def setup_inputs(seed: int = 0) -> dict:
    streams_of = jax.random.split(jax.random.key(seed), 9)
    owners_keys = jax.random.split(jax.random.fold_in(streams_of[0], 1), NUNITS // NUNITS)
    owners_turns = jax.random.permutation(jax.random.fold_in(streams_of[0], 3), NUNITS // NUNITS)
    owners = jax.vmap(lambda own, number: shared_out(jax.random.fold_in(streams_of[0], 2), own, number, NUNITS, N_OWN, 1, SLOTS, 2))(owners_keys, owners_turns).reshape((NUNITS, 1))
    inner_dense = bell_draw(streams_of[1], (GROUPS, NUNITS, UR * D), 1.0, 6.0, ((0, 4), (2, 128)), jnp.float32)
    anchor_dense = bell_draw(streams_of[2], (NUNITS, UR * D), 1.0, 6.0, ((1, 128),), jnp.float32)
    momentum_dense = bell_draw(streams_of[3], (N_OWN * SLOTS, UR * D), 1.0, 6.0, ((0, 128),), jnp.float32)
    inner_emb = bell_draw(streams_of[4], (GROUPS, VOCAB, D), 1.0, 6.0, ((0, 4), (1, 128)), jnp.float32)
    anchor_emb = bell_draw(streams_of[5], (VOCAB, D), 1.0, 6.0, ((0, 128),), jnp.float32)
    momentum_emb = bell_draw(streams_of[6], (VOCAB, RANK), 1.0, 6.0, ((0, 128),), jnp.float32)
    basis = bell_draw(streams_of[7], (D, RANK), D ** -0.5, 0.1875, (), jnp.float32)
    return dict(owners=owners, inner_dense=inner_dense, anchor_dense=anchor_dense, momentum_dense=momentum_dense, inner_emb=inner_emb, anchor_emb=anchor_emb, momentum_emb=momentum_emb, basis=basis)


outer_rate = 0.7
momentum_decay = 0.9


def reference(owners, inner_dense, anchor_dense, momentum_dense, inner_emb, anchor_emb, momentum_emb, basis):
    owner_flat = owners[:, 0].astype(jnp.int32)
    onehot = (owner_flat[:, None] == jnp.arange(N_OWN, dtype=jnp.int32)[None, :]).astype(jnp.int32)
    running = jnp.cumsum(onehot, axis=0) - onehot
    slot_of = jnp.sum(running * onehot, axis=1).astype(jnp.int32)
    row_index = owner_flat * SLOTS + slot_of
    summed = jnp.zeros_like(anchor_dense)
    for group in range(GROUPS):
        summed = summed + (anchor_dense - inner_dense[group])
    mean_grad = summed / GROUPS
    grad_slots = jnp.zeros(momentum_dense.shape, anchor_dense.dtype).at[row_index].set(mean_grad)
    live_rows = jnp.zeros((momentum_dense.shape[0],), jnp.int32).at[row_index].set(1)
    new_momentum_dense = jnp.where(live_rows[:, None] > 0, momentum_decay * momentum_dense + grad_slots, 0.0)
    update = mean_grad + momentum_decay * new_momentum_dense[row_index]
    new_dense = anchor_dense - outer_rate * update
    factor_sum = jnp.zeros(momentum_emb.shape, anchor_emb.dtype)
    for group in range(GROUPS):
        factor_sum = factor_sum + jnp.dot(anchor_emb - inner_emb[group], basis, precision=lax.Precision.HIGHEST, preferred_element_type=jnp.float32)
    mean_factor = factor_sum / GROUPS
    new_momentum_emb = momentum_decay * momentum_emb + mean_factor
    emb_update = mean_factor + momentum_decay * new_momentum_emb
    new_emb = anchor_emb - outer_rate * jnp.dot(emb_update, basis.T, precision=lax.Precision.HIGHEST, preferred_element_type=jnp.float32)
    return (new_dense, new_momentum_dense, new_emb, new_momentum_emb)
```

```python
import jax
import jax.numpy as jnp
from jax import lax
from jax.experimental import pallas as pl
from jax.experimental.pallas import tpu as pltpu
from jax.sharding import PartitionSpec as P

MESH = pl.DeviceIdType.MESH
RATE = 0.7
DECAY = 0.9
NX, NZ, NC, NR, NS = 4, 16, 2, 4, 4
LANES = 128
F32 = jnp.float32
BF16 = jnp.bfloat16
SEND_ORDER = (8, 7, 9, 6, 10, 5, 11, 4, 12, 3, 13, 2, 14, 1, 15)
RANGES = ((6, 11), (3, 6), (11, 14), (14, 16), (0, 3))
GROUPS_Z = ((0,), (1, 2), (3, 4))


def split3(v):
    high = v.astype(BF16)
    rest = v - high.astype(F32)
    mid = rest.astype(BF16)
    low = (rest - mid.astype(F32)).astype(BF16)
    return high, mid, low


def select_rows(onehot, v):
    high, mid, low = split3(v)
    total = jnp.dot(onehot, low, preferred_element_type=F32)
    total = total + jnp.dot(onehot, mid, preferred_element_type=F32)
    return total + jnp.dot(onehot, high, preferred_element_type=F32)


def kernel(
    owners_hbm, inner_hbm, anchor_hbm, mom_hbm, iemb_hbm, aemb_hbm, memb_hbm, basis_hbm,
    nd_out, nm_out, ne_out, nme_out,
    owners, inq, anq, mom_v, ie, ae, memb, basis,
    rly, yin, gq, pack1, pick1, m1, m2, g0, g1, g2, fac,
    loc, rs_recv, mz_recv, mp_recv, gz_recv, gp_recv, gy_recv, gf_recv, nd_recv, f_recv, snd,
):
    own = lax.axis_index("own")
    rep = lax.axis_index("rep")
    c = lax.rem(own, NC)
    z = lax.rem(lax.div(own, NC), NZ)
    x = lax.div(own, NC * NZ)

    def position(px, pz, pc):
        return (px * NZ + pz) * NC + pc

    up = lax.rem(rep + 1, NR)
    down = lax.rem(rep + NR - 1, NR)
    across = lax.rem(rep + 2, NR)
    z_at = [lax.rem(z + d, NZ) for d in range(NZ)]
    z_peers = {d: {"rep": rep, "own": position(x, z_at[d], c)} for d in SEND_ORDER}
    plane = []
    for dx in range(NX):
        for dc in range(NC):
            if dx or dc:
                px, pc = lax.rem(x + dx, NX), lax.rem(c + dc, NC)
                plane.append((px, pc, {"rep": rep, "own": position(px, z, pc)}))
    to_up = {"rep": up, "own": own}
    to_down = {"rep": down, "own": own}
    to_across = {"rep": across, "own": own}

    def local(src, dst, sem):
        copy = pltpu.make_async_copy(src, dst, sem)
        copy.start()

    def arrived(ref, sem):
        pltpu.make_async_copy(ref, ref, sem).wait()

    def send(src, dst, send_sem, recv_sem, peer):
        pltpu.make_async_remote_copy(
            src_ref=src, dst_ref=dst, send_sem=send_sem, recv_sem=recv_sem,
            device_id=peer, device_id_type=MESH,
        ).start()

    def columns(r):
        return pl.ds(pl.multiple_of(r * LANES, LANES), LANES)

    half = (pl.ds(0, 128), pl.ds(128, 128))

    barrier = pltpu.get_barrier_semaphore()
    everyone = [z_peers[d] for d in SEND_ORDER] + [p[2] for p in plane]
    everyone += [to_up, to_down, to_across]
    for peer in everyone:
        pl.semaphore_signal(barrier, inc=1, device_id=peer, device_id_type=MESH)

    local(owners_hbm, owners, loc.at[0])
    local(inner_hbm.at[:, columns(rep)], inq, loc.at[1])
    local(anchor_hbm.at[:, columns(rep)], anq, loc.at[2])
    local(mom_hbm.at[:, z, :, rep], m1.at[0], mz_recv.at[4])
    local(iemb_hbm, ie, loc.at[4])
    local(aemb_hbm, ae, loc.at[5])
    local(basis_hbm, basis, loc.at[6])
    local(memb_hbm, memb, loc.at[7])
    local(mom_hbm, mom_v, loc.at[3])

    pl.semaphore_wait(barrier, len(everyone))

    send(inner_hbm.at[half[0], columns(across)], rly.at[0], snd.at[0], rs_recv.at[0], to_up)
    send(inner_hbm.at[half[1], columns(across)], rly.at[1], snd.at[0], rs_recv.at[1], to_down)
    send(inner_hbm.at[:, columns(up)], yin.at[0], snd.at[1], rs_recv.at[2], to_up)
    send(inner_hbm.at[:, columns(down)], yin.at[1], snd.at[1], rs_recv.at[3], to_down)

    def range_of(d):
        return next(i for i, (a, b) in enumerate(RANGES) if a <= d < b)

    for d in SEND_ORDER:
        send(mom_hbm.at[:, z_at[d], :, rep], m1.at[d], snd.at[2], mz_recv.at[range_of(d)], z_peers[d])

    arrived(owners, loc.at[0])
    names = owners[...]
    by_column = jnp.broadcast_to(names, (256, 256))
    by_row = by_column.T
    first = lax.broadcasted_iota(jnp.int32, (256, 256), 0)
    second = lax.broadcasted_iota(jnp.int32, (256, 256), 1)
    same = by_row == by_column
    slot_row = jnp.sum(jnp.where(same & (first < second), 1, 0), axis=0, keepdims=True)
    slot_column = jnp.sum(jnp.where(same & (second < first), 1, 0), axis=1, keepdims=True)

    def parts(p):
        return p >> 5, (p >> 1) & 15, p & 1

    ox, oz, oc = parts(names)
    pack_row = ((((oz - z) & 15) * NX + ox) * NC + oc) * NS + slot_row
    pack1[...] = jnp.where(
        lax.broadcasted_iota(jnp.int32, (512, 256), 0) == pack_row, 1.0, 0.0
    ).astype(BF16)
    ox, oz, oc = parts(by_row[:, 0:1])
    pick_column = ((ox * NZ + ((z - oz) & 15)) * NC + oc) * NS + slot_column
    pick1[...] = jnp.where(
        lax.broadcasted_iota(jnp.int32, (256, 512), 1) == pick_column, 1.0, 0.0
    ).astype(BF16)
    owned = jnp.sum(jnp.where(names == own, 1, 0), axis=1, keepdims=True)

    arrived(rly.at[0], rs_recv.at[0])
    send(rly.at[0], yin.at[2, half[0]], snd.at[3], rs_recv.at[4], to_up)
    arrived(rly.at[1], rs_recv.at[1])
    send(rly.at[1], yin.at[2, half[1]], snd.at[3], rs_recv.at[5], to_down)

    arrived(ie, loc.at[4])
    arrived(ae, loc.at[5])
    arrived(basis, loc.at[6])
    fac[rep] = lax.dot_general(
        basis[...], ae[...] - ie[...], (((1,), (1,)), ((), ())),
        precision=lax.Precision.HIGHEST, preferred_element_type=F32,
    )

    arrived(inq, loc.at[1])
    arrived(anq, loc.at[2])
    arrived(yin.at[0], rs_recv.at[2])
    arrived(yin.at[1], rs_recv.at[3])
    arrived(yin.at[2, half[0]], rs_recv.at[4])
    arrived(yin.at[2, half[1]], rs_recv.at[5])
    anchor = anq[...]
    grad = (anchor - inq[...]) + (anchor - yin[0])
    grad = (grad + (anchor - yin[1]) + (anchor - yin[2])) * 0.25
    gq[...] = grad
    g0[...] = select_rows(pack1[...], grad).reshape(NZ, NX, NC, NS, LANES)
    for d in SEND_ORDER:
        send(g0.at[d], g1.at[d], snd.at[4], gz_recv.at[range_of(d)], z_peers[d])
    local(g0.at[0], g1.at[0], gz_recv.at[4])
    for i, peer in enumerate((to_up, to_down, to_across)):
        send(fac.at[rep], fac.at[rep], snd.at[5], f_recv.at[i], peer)

    def spread(src, dst, i, send_sem, recv_sem):
        run = pl.ds(RANGES[i][0], RANGES[i][1] - RANGES[i][0])
        for px, pc, peer in plane:
            send(src.at[run, px, pc], dst.at[x, run, c], send_sem, recv_sem, peer)
        local(src.at[run, x, c], dst.at[x, run, c], recv_sem)

    def run_of(i):
        return pl.ds(RANGES[i][0], RANGES[i][1] - RANGES[i][0])

    def m_group(group):
        for i in GROUPS_Z[group]:
            arrived(m1.at[run_of(i)], mz_recv.at[i])
            spread(m1, m2, i, snd.at[6], mp_recv.at[i])

    def g_group(group):
        for i in GROUPS_Z[group]:
            arrived(g1.at[run_of(i)], gz_recv.at[i])
            spread(g1, g2.at[rep], i, snd.at[7], gp_recv.at[i])

    for group in range(3):
        m_group(group)
    for i in range(len(RANGES)):
        arrived(m2.at[:, run_of(i)], mp_recv.at[i])
    momentum = select_rows(pick1[...], m2[...].reshape(512, LANES))
    grad = gq[...]
    nd_out[:, columns(rep)] = anq[...] - RATE * (grad + DECAY * (DECAY * momentum + grad))

    def nd_part(r, h):
        return nd_out.at[half[h], columns(r)]

    send(nd_part(rep, 0), nd_part(rep, 0), snd.at[8], nd_recv.at[0], to_up)
    send(nd_part(rep, 1), nd_part(rep, 1), snd.at[8], nd_recv.at[3], to_down)
    send(nd_part(rep, 1), nd_part(rep, 1), snd.at[8], nd_recv.at[1], to_up)
    send(nd_part(rep, 0), nd_part(rep, 0), snd.at[8], nd_recv.at[2], to_down)

    arrived(memb, loc.at[7])
    arrived(fac.at[down], f_recv.at[0])
    arrived(fac.at[up], f_recv.at[1])
    arrived(fac.at[across], f_recv.at[2])
    mean_factor = ((fac[0] + fac[1]) + (fac[2] + fac[3])) * 0.25
    new_memb = DECAY * memb[...] + mean_factor
    nme_out[...] = new_memb
    emb_update = mean_factor + DECAY * new_memb
    ne_out[...] = ae[...] - RATE * lax.dot_general(
        emb_update, basis[...], (((0,), (0,)), ((), ())),
        precision=lax.Precision.HIGHEST, preferred_element_type=F32,
    )

    g_group(0)
    arrived(nd_part(down, 0), nd_recv.at[0])
    send(nd_part(down, 0), nd_part(down, 0), snd.at[9], nd_recv.at[4], to_up)
    arrived(nd_part(up, 1), nd_recv.at[3])
    send(nd_part(up, 1), nd_part(up, 1), snd.at[9], nd_recv.at[5], to_down)

    def g_part(r, i, h):
        return g2.at[r, pl.ds(2 * h, 2), run_of(i)]

    def g_share(group):
        for i in GROUPS_Z[group]:
            arrived(g2.at[rep, :, run_of(i)], gp_recv.at[i])
            send(g_part(rep, i, 0), g_part(rep, i, 0), snd.at[10], gy_recv.at[i, 0], to_up)
            send(g_part(rep, i, 1), g_part(rep, i, 1), snd.at[10], gy_recv.at[i, 3], to_down)
            send(g_part(rep, i, 1), g_part(rep, i, 1), snd.at[10], gy_recv.at[i, 1], to_up)
            send(g_part(rep, i, 0), g_part(rep, i, 0), snd.at[10], gy_recv.at[i, 2], to_down)

    def g_relay(group):
        for i in GROUPS_Z[group]:
            arrived(g_part(down, i, 0), gy_recv.at[i, 0])
            send(g_part(down, i, 0), g_part(down, i, 0), snd.at[11], gf_recv.at[i, 0], to_up)
            arrived(g_part(up, i, 1), gy_recv.at[i, 3])
            send(g_part(up, i, 1), g_part(up, i, 1), snd.at[11], gf_recv.at[i, 1], to_down)

    g_group(1)
    g_share(0)
    g_group(2)
    g_share(1)
    g_relay(0)
    g_share(2)
    g_relay(1)
    g_relay(2)

    arrived(nd_part(down, 1), nd_recv.at[1])
    arrived(nd_part(up, 0), nd_recv.at[2])
    arrived(nd_part(across, 0), nd_recv.at[4])
    arrived(nd_part(across, 1), nd_recv.at[5])
    arrived(mom_v, loc.at[3])
    for i in range(len(RANGES)):
        arrived(g_part(down, i, 1), gy_recv.at[i, 1])
        arrived(g_part(up, i, 0), gy_recv.at[i, 2])
        arrived(g_part(across, i, 0), gf_recv.at[i, 0])
        arrived(g_part(across, i, 1), gf_recv.at[i, 1])

    live = lax.broadcasted_iota(jnp.int32, (NS, LANES), 0) < owned

    def finish(d, carry):
        at = lax.rem(z + NZ - d, NZ)
        for px in range(NX):
            for pc in range(NC):
                for r in range(NR):
                    value = DECAY * mom_v[px, at, pc, r] + g2[r, px, d, pc]
                    nm_out[px, at, pc, r] = jnp.where(live, value, 0.0)
        return carry

    lax.fori_loop(0, NZ, finish, 0)

    arrived(rly, snd.at[0])
    arrived(yin.at[pl.ds(0, 2)], snd.at[1])
    arrived(m1.at[pl.ds(1, 15)], snd.at[2])
    arrived(rly, snd.at[3])
    arrived(g1.at[pl.ds(1, 15)], snd.at[4])
    arrived(fac.at[pl.ds(0, 3)], snd.at[5])
    arrived(m2.at[:, :, 0], snd.at[6])
    arrived(m2.at[pl.ds(0, 3), :, 0], snd.at[6])
    arrived(m2.at[:, :, 0], snd.at[7])
    arrived(m2.at[pl.ds(0, 3), :, 0], snd.at[7])
    arrived(yin.at[pl.ds(0, 2)], snd.at[8])
    arrived(rly, snd.at[9])
    arrived(g2.at[pl.ds(0, 2)], snd.at[10])
    arrived(g2.at[0], snd.at[11])


def per_device(
    owners, inner_dense, anchor_dense, momentum_dense, inner_emb, anchor_emb, momentum_emb, basis
):
    mom = momentum_dense.reshape(NS, 512, LANES).transpose(1, 0, 2)
    mom = mom.reshape(NX, NZ, NC, NR, NS, LANES)
    dma = pltpu.SemaphoreType.DMA
    vmem = pltpu.VMEM
    vocab, width = anchor_emb.shape
    rank = basis.shape[1]
    ranges = len(RANGES)
    new_dense, new_mom, new_emb, new_memb = pl.pallas_call(
        kernel,
        out_shape=(
            jax.ShapeDtypeStruct(anchor_dense.shape, F32),
            jax.ShapeDtypeStruct(mom.shape, F32),
            jax.ShapeDtypeStruct(anchor_emb.shape, F32),
            jax.ShapeDtypeStruct((rank, vocab), F32),
        ),
        in_specs=[pl.BlockSpec(memory_space=pltpu.HBM)] * 8,
        out_specs=[pl.BlockSpec(memory_space=pltpu.VMEM)] * 4,
        scratch_shapes=[
            vmem((1, 256), jnp.int32),
            vmem((256, LANES), F32),
            vmem((256, LANES), F32),
            vmem(mom.shape, F32),
            vmem((vocab, width), F32),
            vmem((vocab, width), F32),
            vmem((rank, vocab), F32),
            vmem((rank, width), F32),
            vmem((2, 128, LANES), F32),
            vmem((3, 256, LANES), F32),
            vmem((256, LANES), F32),
            vmem((512, 256), BF16),
            vmem((256, 512), BF16),
            vmem((NZ, NX, NC, NS, LANES), F32),
            vmem((NX, NZ, NC, NS, LANES), F32),
            vmem((NZ, NX, NC, NS, LANES), F32),
            vmem((NZ, NX, NC, NS, LANES), F32),
            vmem((NR, NX, NZ, NC, NS, LANES), F32),
            vmem((NR, rank, vocab), F32),
            dma((8,)),
            dma((6,)),
            dma((ranges,)),
            dma((ranges,)),
            dma((ranges,)),
            dma((ranges,)),
            dma((ranges, 4)),
            dma((ranges, 2)),
            dma((6,)),
            dma((3,)),
            dma((12,)),
        ],
        compiler_params=pltpu.CompilerParams(
            collective_id=0, has_side_effects=True, vmem_limit_bytes=32 * 1024 * 1024
        ),
    )(
        owners.reshape(1, 256), inner_dense[0], anchor_dense, mom, inner_emb[0], anchor_emb,
        momentum_emb.T, basis.T,
    )
    new_mom = new_mom.reshape(512, NS, LANES).transpose(1, 0, 2).reshape(momentum_dense.shape)
    return new_dense, new_mom, new_emb, new_memb.T


def solution(mesh):
    placed = (
        P(),
        P("rep", None, "own"),
        P(None, "own"),
        P("own", None),
        P("rep", "own", None),
        P("own", None),
        P("own", None),
        P(),
    )
    return jax.shard_map(
        per_device,
        mesh=mesh,
        in_specs=placed,
        out_specs=(P(None, "own"), P("own", None), P("own", None), P("own", None)),
        check_vma=False,
    )
```

```python
import jax
import jax.numpy as jnp
from jax import lax
from jax.experimental import pallas as pl
from jax.experimental.pallas import tpu as pltpu
from jax.sharding import PartitionSpec as P

MESH = pl.DeviceIdType.MESH
RATE = 0.7
DECAY = 0.9
NX, NZ, NC, NR, NS = 4, 16, 2, 4, 4
LANES = 128
F32 = jnp.float32
BF16 = jnp.bfloat16
DISTANCE = (0, 1, 15, 2, 14, 3, 13, 4, 12, 5, 11, 6, 10, 7, 9, 8)
M_GROUPS = ((13, 16), (9, 13), (0, 9))
G_GROUPS = ((0, 5), (5, 9), (9, 13), (13, 16))
G_PLANE = ((0, 9), (9, 16))


def split3(v):
    high = v.astype(BF16)
    rest = v - high.astype(F32)
    mid = rest.astype(BF16)
    low = (rest - mid.astype(F32)).astype(BF16)
    return high, mid, low


def select_rows(onehot, v):
    high, mid, low = split3(v)
    total = jnp.dot(onehot, low, preferred_element_type=F32)
    total = total + jnp.dot(onehot, mid, preferred_element_type=F32)
    return total + jnp.dot(onehot, high, preferred_element_type=F32)


def slot_of_distance(e):
    e = ((e + 8) & 15) - 8
    return jnp.minimum(jnp.where(e > 0, 2 * e - 1, -2 * e), 15)


def kernel(
    owners_hbm, inner_hbm, anchor_hbm, mom_hbm, iemb_hbm, aemb_hbm, memb_hbm, basis_hbm,
    nd_out, nm_out, ne_out, nme_out,
    owners, inq, anq, mom_v, ie, ae, memb, basis,
    rly, yin, gq, pack1, pick1, m1, m2, g0, g1, g2, fac,
    loc, rs_recv, mz_recv, mp_recv, gp_recv, gz_recv, gy_recv, gf_recv, nd_recv, f_recv, snd,
):
    own = lax.axis_index("own")
    rep = lax.axis_index("rep")
    c = lax.rem(own, NC)
    z = lax.rem(lax.div(own, NC), NZ)
    x = lax.div(own, NC * NZ)

    def position(px, pz, pc):
        return (px * NZ + pz) * NC + pc

    up = lax.rem(rep + 1, NR)
    down = lax.rem(rep + NR - 1, NR)
    across = lax.rem(rep + 2, NR)
    z_at = [lax.rem(z + d, NZ) for d in DISTANCE]
    z_peers = [{"rep": rep, "own": position(x, at, c)} for at in z_at]
    plane = []
    for dx in range(NX):
        for dc in range(NC):
            if dx or dc:
                px, pc = lax.rem(x + dx, NX), lax.rem(c + dc, NC)
                plane.append((px, pc, {"rep": rep, "own": position(px, z, pc)}))
    to_up = {"rep": up, "own": own}
    to_down = {"rep": down, "own": own}
    to_across = {"rep": across, "own": own}

    def local(src, dst, sem):
        copy = pltpu.make_async_copy(src, dst, sem)
        copy.start()

    def arrived(ref, sem):
        pltpu.make_async_copy(ref, ref, sem).wait()

    def send(src, dst, send_sem, recv_sem, peer):
        pltpu.make_async_remote_copy(
            src_ref=src, dst_ref=dst, send_sem=send_sem, recv_sem=recv_sem,
            device_id=peer, device_id_type=MESH,
        ).start()

    def columns(r):
        return pl.ds(pl.multiple_of(r * LANES, LANES), LANES)

    def run(ends):
        return pl.ds(ends[0], ends[1] - ends[0])

    half = (pl.ds(0, 128), pl.ds(128, 128))

    barrier = pltpu.get_barrier_semaphore()
    everyone = z_peers[1:] + [p[2] for p in plane] + [to_up, to_down, to_across]
    for peer in everyone:
        pl.semaphore_signal(barrier, inc=1, device_id=peer, device_id_type=MESH)

    local(owners_hbm, owners, loc.at[0])
    local(inner_hbm.at[:, columns(rep)], inq, loc.at[1])
    local(anchor_hbm.at[:, columns(rep)], anq, loc.at[2])
    local(mom_hbm.at[:, z, :, rep], m1.at[0], mz_recv.at[2])
    local(iemb_hbm, ie, loc.at[4])
    local(aemb_hbm, ae, loc.at[5])
    local(basis_hbm, basis, loc.at[6])
    local(memb_hbm, memb, loc.at[7])
    local(mom_hbm, mom_v, loc.at[3])

    pl.semaphore_wait(barrier, len(everyone))

    send(inner_hbm.at[half[0], columns(across)], rly.at[0], snd.at[0], rs_recv.at[0], to_up)
    send(inner_hbm.at[half[1], columns(across)], rly.at[1], snd.at[0], rs_recv.at[1], to_down)
    send(inner_hbm.at[:, columns(up)], yin.at[0], snd.at[1], rs_recv.at[2], to_up)
    send(inner_hbm.at[:, columns(down)], yin.at[1], snd.at[1], rs_recv.at[3], to_down)

    for group, (low, high) in enumerate(M_GROUPS):
        for k in reversed(range(max(low, 1), high)):
            send(mom_hbm.at[:, z_at[k], :, rep], m1.at[k], snd.at[2], mz_recv.at[group], z_peers[k])

    arrived(owners, loc.at[0])
    names = owners[...]
    by_column = jnp.broadcast_to(names, (256, 256))
    by_row = by_column.T
    first = lax.broadcasted_iota(jnp.int32, (256, 256), 0)
    second = lax.broadcasted_iota(jnp.int32, (256, 256), 1)
    same = by_row == by_column
    slot_row = jnp.sum(jnp.where(same & (first < second), 1, 0), axis=0, keepdims=True)
    slot_column = jnp.sum(jnp.where(same & (second < first), 1, 0), axis=1, keepdims=True)

    def parts(p):
        return p >> 5, (p >> 1) & 15, p & 1

    ox, oz, oc = parts(names)
    pack_row = ((ox * NC + oc) * NZ + slot_of_distance(oz - z)) * NS + slot_row
    pack1[...] = jnp.where(
        lax.broadcasted_iota(jnp.int32, (512, 256), 0) == pack_row, 1.0, 0.0
    ).astype(BF16)
    ox, oz, oc = parts(by_row[:, 0:1])
    pick_column = ((ox * NC + oc) * NZ + slot_of_distance(z - oz)) * NS + slot_column
    pick1[...] = jnp.where(
        lax.broadcasted_iota(jnp.int32, (256, 512), 1) == pick_column, 1.0, 0.0
    ).astype(BF16)
    owned = jnp.sum(jnp.where(names == own, 1, 0), axis=1, keepdims=True)

    arrived(rly.at[0], rs_recv.at[0])
    send(rly.at[0], yin.at[2, half[0]], snd.at[3], rs_recv.at[4], to_up)
    arrived(rly.at[1], rs_recv.at[1])
    send(rly.at[1], yin.at[2, half[1]], snd.at[3], rs_recv.at[5], to_down)

    arrived(ie, loc.at[4])
    arrived(ae, loc.at[5])
    arrived(basis, loc.at[6])
    fac[rep] = lax.dot_general(
        basis[...], ae[...] - ie[...], (((1,), (1,)), ((), ())),
        precision=lax.Precision.HIGHEST, preferred_element_type=F32,
    )

    arrived(inq, loc.at[1])
    arrived(anq, loc.at[2])
    arrived(yin.at[0], rs_recv.at[2])
    arrived(yin.at[1], rs_recv.at[3])
    arrived(yin.at[2, half[0]], rs_recv.at[4])
    arrived(yin.at[2, half[1]], rs_recv.at[5])
    anchor = anq[...]
    grad = (anchor - inq[...]) + (anchor - yin[0])
    grad = (grad + (anchor - yin[1]) + (anchor - yin[2])) * 0.25
    gq[...] = grad
    g0[...] = select_rows(pack1[...], grad).reshape(NX, NC, NZ, NS, LANES)
    for i, ends in enumerate(G_PLANE):
        for px, pc, peer in plane:
            send(g0.at[px, pc, run(ends)], g1.at[x, c, run(ends)], snd.at[4], gp_recv.at[i], peer)
        local(g0.at[x, c, run(ends)], g1.at[x, c, run(ends)], gp_recv.at[i])
    for i, peer in enumerate((to_up, to_down, to_across)):
        send(fac.at[rep], fac.at[rep], snd.at[5], f_recv.at[i], peer)

    def m_group(group):
        ends = M_GROUPS[group]
        arrived(m1.at[run(ends)], mz_recv.at[group])
        for px, pc, peer in plane:
            send(m1.at[run(ends), px, pc], m2.at[x, c, run(ends)], snd.at[6], mp_recv.at[group], peer)
        local(m1.at[run(ends), x, c], m2.at[x, c, run(ends)], mp_recv.at[group])

    m_group(0)
    m_group(1)
    group_of = [next(i for i, (a, b) in enumerate(G_GROUPS) if a <= k < b) for k in range(NZ)]
    for i, ends in enumerate(G_PLANE):
        arrived(g1.at[:, :, run(ends)], gp_recv.at[i])
        for k in range(max(ends[0], 1), ends[1]):
            send(g1.at[:, :, k], g2.at[rep, k], snd.at[7], gz_recv.at[group_of[k]], z_peers[k])
        if i == 0:
            local(g1.at[:, :, 0], g2.at[rep, 0], gz_recv.at[0])
    m_group(2)

    for group, ends in enumerate(M_GROUPS):
        arrived(m2.at[:, :, run(ends)], mp_recv.at[group])
    momentum = select_rows(pick1[...], m2[...].reshape(512, LANES))
    grad = gq[...]
    nd_out[:, columns(rep)] = anq[...] - RATE * (grad + DECAY * (DECAY * momentum + grad))

    def nd_part(r, h):
        return nd_out.at[half[h], columns(r)]

    send(nd_part(rep, 0), nd_part(rep, 0), snd.at[8], nd_recv.at[0], to_up)
    send(nd_part(rep, 1), nd_part(rep, 1), snd.at[8], nd_recv.at[3], to_down)
    send(nd_part(rep, 1), nd_part(rep, 1), snd.at[8], nd_recv.at[1], to_up)
    send(nd_part(rep, 0), nd_part(rep, 0), snd.at[8], nd_recv.at[2], to_down)

    def g_part(r, group, h):
        return g2.at[r, run(G_GROUPS[group]), pl.ds(2 * h, 2)]

    def g_share(group):
        arrived(g2.at[rep, run(G_GROUPS[group])], gz_recv.at[group])
        for h, sem, peer in ((0, 0, to_up), (1, 3, to_down), (1, 1, to_up), (0, 2, to_down)):
            part = g_part(rep, group, h)
            send(part, part, snd.at[10], gy_recv.at[group, sem], peer)

    def g_relay(group):
        arrived(g_part(down, group, 0), gy_recv.at[group, 0])
        send(g_part(down, group, 0), g_part(down, group, 0), snd.at[11], gf_recv.at[group, 0], to_up)
        arrived(g_part(up, group, 1), gy_recv.at[group, 3])
        send(g_part(up, group, 1), g_part(up, group, 1), snd.at[11], gf_recv.at[group, 1], to_down)

    g_share(0)

    arrived(memb, loc.at[7])
    arrived(fac.at[down], f_recv.at[0])
    arrived(fac.at[up], f_recv.at[1])
    arrived(fac.at[across], f_recv.at[2])
    mean_factor = ((fac[0] + fac[1]) + (fac[2] + fac[3])) * 0.25
    new_memb = DECAY * memb[...] + mean_factor
    nme_out[...] = new_memb
    emb_update = mean_factor + DECAY * new_memb
    ne_out[...] = ae[...] - RATE * lax.dot_general(
        emb_update, basis[...], (((0,), (0,)), ((), ())),
        precision=lax.Precision.HIGHEST, preferred_element_type=F32,
    )

    arrived(nd_part(down, 0), nd_recv.at[0])
    send(nd_part(down, 0), nd_part(down, 0), snd.at[9], nd_recv.at[4], to_up)
    arrived(nd_part(up, 1), nd_recv.at[3])
    send(nd_part(up, 1), nd_part(up, 1), snd.at[9], nd_recv.at[5], to_down)
    g_relay(0)
    for group in range(1, len(G_GROUPS)):
        g_share(group)
        if group > 1:
            g_relay(group - 1)
    g_relay(len(G_GROUPS) - 1)

    arrived(nd_part(down, 1), nd_recv.at[1])
    arrived(nd_part(up, 0), nd_recv.at[2])
    arrived(nd_part(across, 0), nd_recv.at[4])
    arrived(nd_part(across, 1), nd_recv.at[5])
    arrived(mom_v, loc.at[3])
    live = lax.broadcasted_iota(jnp.int32, (NS, LANES), 0) < owned

    def finish(k, carry):
        steps = lax.div(k + 1, 2)
        at = lax.rem(z + NZ + (1 - 2 * lax.rem(k, 2)) * steps, NZ)
        for px in range(NX):
            for pc in range(NC):
                for r in range(NR):
                    value = DECAY * mom_v[px, at, pc, r] + g2[r, k, px, pc]
                    nm_out[px, at, pc, r] = jnp.where(live, value, 0.0)
        return carry

    for group, ends in enumerate(G_GROUPS):
        arrived(g_part(down, group, 1), gy_recv.at[group, 1])
        arrived(g_part(up, group, 0), gy_recv.at[group, 2])
        arrived(g_part(across, group, 0), gf_recv.at[group, 0])
        arrived(g_part(across, group, 1), gf_recv.at[group, 1])
        lax.fori_loop(ends[0], ends[1], finish, 0)

    arrived(rly, snd.at[0])
    arrived(yin.at[pl.ds(0, 2)], snd.at[1])
    arrived(m1.at[pl.ds(1, 15)], snd.at[2])
    arrived(rly, snd.at[3])
    arrived(m1.at[pl.ds(0, 14)], snd.at[4])
    arrived(fac.at[pl.ds(0, 3)], snd.at[5])
    arrived(m1.at[pl.ds(0, 14)], snd.at[6])
    arrived(m1.at[pl.ds(1, 15)], snd.at[7])
    arrived(yin.at[pl.ds(0, 2)], snd.at[8])
    arrived(rly, snd.at[9])
    arrived(g2.at[pl.ds(0, 2)], snd.at[10])
    arrived(g2.at[0], snd.at[11])


def store_out(*refs):
    count = len(refs) // 2
    sem = refs[-1]
    copies = [pltpu.make_async_copy(refs[i], refs[count + i], sem.at[i]) for i in range(count)]
    for copy in copies:
        copy.start()
    for copy in copies:
        copy.wait()


def per_device(
    owners, inner_dense, anchor_dense, momentum_dense, inner_emb, anchor_emb, momentum_emb, basis
):
    mom = momentum_dense.reshape(NS, 512, LANES).transpose(1, 0, 2)
    mom = mom.reshape(NX, NZ, NC, NR, NS, LANES)
    dma = pltpu.SemaphoreType.DMA
    vmem = pltpu.VMEM
    vocab, width = anchor_emb.shape
    rank = basis.shape[1]
    results = pl.pallas_call(
        kernel,
        out_shape=(
            jax.ShapeDtypeStruct(anchor_dense.shape, F32),
            jax.ShapeDtypeStruct(mom.shape, F32),
            jax.ShapeDtypeStruct(anchor_emb.shape, F32),
            jax.ShapeDtypeStruct((rank, vocab), F32),
        ),
        in_specs=[pl.BlockSpec(memory_space=pltpu.HBM)] * 8,
        out_specs=[pl.BlockSpec(memory_space=pltpu.VMEM)] * 4,
        scratch_shapes=[
            vmem((1, 256), jnp.int32),
            vmem((256, LANES), F32),
            vmem((256, LANES), F32),
            vmem(mom.shape, F32),
            vmem((vocab, width), F32),
            vmem((vocab, width), F32),
            vmem((rank, vocab), F32),
            vmem((rank, width), F32),
            vmem((2, 128, LANES), F32),
            vmem((3, 256, LANES), F32),
            vmem((256, LANES), F32),
            vmem((512, 256), BF16),
            vmem((256, 512), BF16),
            vmem((NZ, NX, NC, NS, LANES), F32),
            vmem((NX, NC, NZ, NS, LANES), F32),
            vmem((NX, NC, NZ, NS, LANES), F32),
            vmem((NX, NC, NZ, NS, LANES), F32),
            vmem((NR, NZ, NX, NC, NS, LANES), F32),
            vmem((NR, rank, vocab), F32),
            dma((8,)),
            dma((6,)),
            dma((len(M_GROUPS),)),
            dma((len(M_GROUPS),)),
            dma((len(G_PLANE),)),
            dma((len(G_GROUPS),)),
            dma((len(G_GROUPS), 4)),
            dma((len(G_GROUPS), 2)),
            dma((6,)),
            dma((3,)),
            dma((12,)),
        ],
        compiler_params=pltpu.CompilerParams(
            collective_id=0, has_side_effects=True, vmem_limit_bytes=32 * 1024 * 1024
        ),
    )(*[
        pltpu.with_memory_space_constraint(v, pltpu.HBM)
        for v in (
            owners.reshape(1, 256), inner_dense[0], anchor_dense, mom, inner_emb[0], anchor_emb,
            momentum_emb.T, basis.T,
        )
    ])
    new_dense, new_mom, new_emb, new_memb = pl.pallas_call(
        store_out,
        out_shape=[jax.ShapeDtypeStruct(v.shape, v.dtype) for v in results],
        in_specs=[pl.BlockSpec(memory_space=pltpu.VMEM)] * 4,
        out_specs=[pl.BlockSpec(memory_space=pltpu.HBM)] * 4,
        scratch_shapes=[dma((4,))],
        compiler_params=pltpu.CompilerParams(vmem_limit_bytes=4 * 1024 * 1024),
    )(*results)
    new_mom = new_mom.reshape(512, NS, LANES).transpose(1, 0, 2).reshape(momentum_dense.shape)
    return new_dense, new_mom, new_emb, new_memb.T


def solution(mesh):
    placed = (
        P(),
        P("rep", None, "own"),
        P(None, "own"),
        P("own", None),
        P("rep", "own", None),
        P("own", None),
        P("own", None),
        P(),
    )
    return jax.shard_map(
        per_device,
        mesh=mesh,
        in_specs=placed,
        out_specs=(P(None, "own"), P("own", None), P("own", None), P("own", None)),
        check_vma=False,
    )
```

```python
import jax
import jax.numpy as jnp
from jax import lax
from jax.experimental import pallas as pl
from jax.experimental.pallas import tpu as pltpu
from jax.sharding import PartitionSpec as P

MESH = pl.DeviceIdType.MESH
RATE = 0.7
DECAY = 0.9
NX, NZ, NC, NR, NS = 4, 16, 2, 4, 4
LANES = 128
F32 = jnp.float32
BF16 = jnp.bfloat16
DISTANCE = (0, 1, 15, 2, 14, 3, 13, 4, 12, 5, 11, 6, 10, 7, 9, 8)
M_GROUPS = ((13, 16), (9, 13), (0, 9))
G_GROUPS = ((0, 5), (5, 9), (9, 13), (13, 15), (15, 16))
G_PLANE = ((0, 5), (5, 16))
DIRECT = 3


def split3(v):
    high = v.astype(BF16)
    rest = v - high.astype(F32)
    mid = rest.astype(BF16)
    low = (rest - mid.astype(F32)).astype(BF16)
    return high, mid, low


def select_rows(onehot, v):
    high, mid, low = split3(v)
    total = jnp.dot(onehot, low, preferred_element_type=F32)
    total = total + jnp.dot(onehot, mid, preferred_element_type=F32)
    return total + jnp.dot(onehot, high, preferred_element_type=F32)


def slot_of_distance(e):
    e = ((e + 8) & 15) - 8
    return jnp.minimum(jnp.where(e > 0, 2 * e - 1, -2 * e), 15)


def kernel(
    owners_hbm, inner_hbm, anchor_hbm, mom_hbm, iemb_hbm, aemb_hbm, memb_hbm, basis_hbm,
    nd_out, nm_out, ne_out, nme_out,
    owners, inq, anq, mom_v, ie, ae, memb, basis,
    rly, yin, gq, pack1, pick1, m1, m2, g0, g1, g2, fac,
    loc, rs_recv, mz_recv, mp_recv, gp_recv, gz_recv, gy_recv, gf_recv, nd_recv, f_recv, snd,
):
    own = lax.axis_index("own")
    rep = lax.axis_index("rep")
    c = lax.rem(own, NC)
    z = lax.rem(lax.div(own, NC), NZ)
    x = lax.div(own, NC * NZ)

    def position(px, pz, pc):
        return (px * NZ + pz) * NC + pc

    up = lax.rem(rep + 1, NR)
    down = lax.rem(rep + NR - 1, NR)
    across = lax.rem(rep + 2, NR)
    z_at = [lax.rem(z + d, NZ) for d in DISTANCE]
    z_peers = [{"rep": rep, "own": position(x, at, c)} for at in z_at]
    plane = []
    for dx in range(NX):
        for dc in range(NC):
            if dx or dc:
                px, pc = lax.rem(x + dx, NX), lax.rem(c + dc, NC)
                plane.append((px, pc, {"rep": rep, "own": position(px, z, pc)}))
    to_up = {"rep": up, "own": own}
    to_down = {"rep": down, "own": own}
    to_across = {"rep": across, "own": own}

    def local(src, dst, sem):
        copy = pltpu.make_async_copy(src, dst, sem)
        copy.start()

    def arrived(ref, sem):
        pltpu.make_async_copy(ref, ref, sem).wait()

    def send(src, dst, send_sem, recv_sem, peer):
        pltpu.make_async_remote_copy(
            src_ref=src, dst_ref=dst, send_sem=send_sem, recv_sem=recv_sem,
            device_id=peer, device_id_type=MESH,
        ).start()

    def columns(r):
        return pl.ds(pl.multiple_of(r * LANES, LANES), LANES)

    def run(ends):
        return pl.ds(ends[0], ends[1] - ends[0])

    half = (pl.ds(0, 128), pl.ds(128, 128))

    barrier = pltpu.get_barrier_semaphore()
    everyone = z_peers[1:] + [p[2] for p in plane] + [to_up, to_down, to_across]
    for peer in everyone:
        pl.semaphore_signal(barrier, inc=1, device_id=peer, device_id_type=MESH)

    local(owners_hbm, owners, loc.at[0])
    local(inner_hbm.at[:, columns(rep)], inq, loc.at[1])
    local(anchor_hbm.at[:, columns(rep)], anq, loc.at[2])
    local(mom_hbm.at[:, z, :, rep], m1.at[0], mz_recv.at[2])
    local(iemb_hbm, ie, loc.at[4])
    local(aemb_hbm, ae, loc.at[5])
    local(basis_hbm, basis, loc.at[6])
    local(memb_hbm, memb, loc.at[7])
    local(mom_hbm, mom_v, loc.at[3])

    pl.semaphore_wait(barrier, len(everyone))

    send(inner_hbm.at[:, columns(across)], yin.at[2], snd.at[1], rs_recv.at[4], to_across)
    send(inner_hbm.at[:, columns(up)], yin.at[0], snd.at[1], rs_recv.at[2], to_up)
    send(inner_hbm.at[:, columns(down)], yin.at[1], snd.at[1], rs_recv.at[3], to_down)

    for group, (low, high) in enumerate(M_GROUPS):
        for k in reversed(range(max(low, 1), high)):
            send(mom_hbm.at[:, z_at[k], :, rep], m1.at[k], snd.at[2], mz_recv.at[group], z_peers[k])

    arrived(owners, loc.at[0])
    names = owners[...]
    by_column = jnp.broadcast_to(names, (256, 256))
    by_row = by_column.T
    first = lax.broadcasted_iota(jnp.int32, (256, 256), 0)
    second = lax.broadcasted_iota(jnp.int32, (256, 256), 1)
    same = by_row == by_column
    slot_row = jnp.sum(jnp.where(same & (first < second), 1, 0), axis=0, keepdims=True)
    slot_column = jnp.sum(jnp.where(same & (second < first), 1, 0), axis=1, keepdims=True)

    def parts(p):
        return p >> 5, (p >> 1) & 15, p & 1

    ox, oz, oc = parts(names)
    pack_row = ((ox * NC + oc) * NZ + slot_of_distance(oz - z)) * NS + slot_row
    pack1[...] = jnp.where(
        lax.broadcasted_iota(jnp.int32, (512, 256), 0) == pack_row, 1.0, 0.0
    ).astype(BF16)
    ox, oz, oc = parts(by_row[:, 0:1])
    pick_column = ((ox * NC + oc) * NZ + slot_of_distance(z - oz)) * NS + slot_column
    pick1[...] = jnp.where(
        lax.broadcasted_iota(jnp.int32, (256, 512), 1) == pick_column, 1.0, 0.0
    ).astype(BF16)
    owned = jnp.sum(jnp.where(names == own, 1, 0), axis=1, keepdims=True)

    arrived(ie, loc.at[4])
    arrived(ae, loc.at[5])
    arrived(basis, loc.at[6])
    fac[rep] = lax.dot_general(
        basis[...], ae[...] - ie[...], (((1,), (1,)), ((), ())),
        precision=lax.Precision.HIGHEST, preferred_element_type=F32,
    )

    arrived(inq, loc.at[1])
    arrived(anq, loc.at[2])
    arrived(yin.at[0], rs_recv.at[2])
    arrived(yin.at[1], rs_recv.at[3])
    arrived(yin.at[2], rs_recv.at[4])
    anchor = anq[...]
    grad = (anchor - inq[...]) + (anchor - yin[0])
    grad = (grad + (anchor - yin[1]) + (anchor - yin[2])) * 0.25
    gq[...] = grad
    g0[...] = select_rows(pack1[...], grad).reshape(NX, NC, NZ, NS, LANES)
    for i, ends in enumerate(G_PLANE):
        for px, pc, peer in plane:
            send(g0.at[px, pc, run(ends)], g1.at[x, c, run(ends)], snd.at[4], gp_recv.at[i], peer)
        local(g0.at[x, c, run(ends)], g1.at[x, c, run(ends)], gp_recv.at[i])
    for i, peer in enumerate((to_up, to_down, to_across)):
        send(fac.at[rep], fac.at[rep], snd.at[5], f_recv.at[i], peer)

    def m_group(group):
        ends = M_GROUPS[group]
        arrived(m1.at[run(ends)], mz_recv.at[group])
        for px, pc, peer in plane:
            send(m1.at[run(ends), px, pc], m2.at[x, c, run(ends)], snd.at[6], mp_recv.at[group], peer)
        local(m1.at[run(ends), x, c], m2.at[x, c, run(ends)], mp_recv.at[group])

    m_group(0)
    m_group(1)
    group_of = [next(i for i, (a, b) in enumerate(G_GROUPS) if a <= k < b) for k in range(NZ)]
    for i, ends in enumerate(G_PLANE):
        arrived(g1.at[:, :, run(ends)], gp_recv.at[i])
        for k in range(max(ends[0], 1), ends[1]):
            send(g1.at[:, :, k], g2.at[rep, k], snd.at[7], gz_recv.at[group_of[k]], z_peers[k])
        if i == 0:
            local(g1.at[:, :, 0], g2.at[rep, 0], gz_recv.at[0])
    m_group(2)

    for group, ends in enumerate(M_GROUPS):
        arrived(m2.at[:, :, run(ends)], mp_recv.at[group])
    momentum = select_rows(pick1[...], m2[...].reshape(512, LANES))
    grad = gq[...]
    nd_out[:, columns(rep)] = anq[...] - RATE * (grad + DECAY * (DECAY * momentum + grad))

    def nd_part(r, h):
        return nd_out.at[half[h], columns(r)]

    send(nd_part(rep, 0), nd_part(rep, 0), snd.at[8], nd_recv.at[0], to_up)
    send(nd_part(rep, 1), nd_part(rep, 1), snd.at[8], nd_recv.at[3], to_down)
    send(nd_part(rep, 1), nd_part(rep, 1), snd.at[8], nd_recv.at[1], to_up)
    send(nd_part(rep, 0), nd_part(rep, 0), snd.at[8], nd_recv.at[2], to_down)

    def g_part(r, group, h):
        return g2.at[r, run(G_GROUPS[group]), pl.ds(2 * h, 2)]

    def g_share(group):
        arrived(g2.at[rep, run(G_GROUPS[group])], gz_recv.at[group])
        if group >= DIRECT:
            whole = g2.at[rep, run(G_GROUPS[group])]
            for sem, peer in ((2, to_across), (0, to_up), (1, to_down)):
                send(whole, whole, snd.at[12], gy_recv.at[group, sem], peer)
            return
        for h, sem, peer in ((0, 0, to_up), (1, 3, to_down), (1, 1, to_up), (0, 2, to_down)):
            part = g_part(rep, group, h)
            send(part, part, snd.at[10], gy_recv.at[group, sem], peer)

    def g_relay(group):
        if group >= DIRECT:
            return
        arrived(g_part(down, group, 0), gy_recv.at[group, 0])
        send(g_part(down, group, 0), g_part(down, group, 0), snd.at[11], gf_recv.at[group, 0], to_up)
        arrived(g_part(up, group, 1), gy_recv.at[group, 3])
        send(g_part(up, group, 1), g_part(up, group, 1), snd.at[11], gf_recv.at[group, 1], to_down)

    g_share(0)

    arrived(memb, loc.at[7])
    arrived(fac.at[down], f_recv.at[0])
    arrived(fac.at[up], f_recv.at[1])
    arrived(fac.at[across], f_recv.at[2])
    mean_factor = ((fac[0] + fac[1]) + (fac[2] + fac[3])) * 0.25
    new_memb = DECAY * memb[...] + mean_factor
    nme_out[...] = new_memb
    emb_update = mean_factor + DECAY * new_memb
    ne_out[...] = ae[...] - RATE * lax.dot_general(
        emb_update, basis[...], (((0,), (0,)), ((), ())),
        precision=lax.Precision.HIGHEST, preferred_element_type=F32,
    )

    arrived(nd_part(down, 0), nd_recv.at[0])
    send(nd_part(down, 0), nd_part(down, 0), snd.at[9], nd_recv.at[4], to_up)
    arrived(nd_part(up, 1), nd_recv.at[3])
    send(nd_part(up, 1), nd_part(up, 1), snd.at[9], nd_recv.at[5], to_down)
    g_relay(0)
    for group in range(1, len(G_GROUPS)):
        g_share(group)
        if group > 1:
            g_relay(group - 1)
    g_relay(len(G_GROUPS) - 1)

    arrived(nd_part(down, 1), nd_recv.at[1])
    arrived(nd_part(up, 0), nd_recv.at[2])
    arrived(nd_part(across, 0), nd_recv.at[4])
    arrived(nd_part(across, 1), nd_recv.at[5])
    arrived(mom_v, loc.at[3])
    live = lax.broadcasted_iota(jnp.int32, (NS, LANES), 0) < owned

    def finish(k, carry):
        steps = lax.div(k + 1, 2)
        at = lax.rem(z + NZ + (1 - 2 * lax.rem(k, 2)) * steps, NZ)
        for px in range(NX):
            for pc in range(NC):
                for r in range(NR):
                    value = DECAY * mom_v[px, at, pc, r] + g2[r, k, px, pc]
                    nm_out[px, at, pc, r] = jnp.where(live, value, 0.0)
        return carry

    for group, ends in enumerate(G_GROUPS):
        if group >= DIRECT:
            for sem, r in enumerate((down, up, across)):
                arrived(g2.at[r, run(ends)], gy_recv.at[group, sem])
        else:
            arrived(g_part(down, group, 1), gy_recv.at[group, 1])
            arrived(g_part(up, group, 0), gy_recv.at[group, 2])
            arrived(g_part(across, group, 0), gf_recv.at[group, 0])
            arrived(g_part(across, group, 1), gf_recv.at[group, 1])
        lax.fori_loop(ends[0], ends[1], finish, 0)

    arrived(yin, snd.at[1])
    arrived(m1.at[pl.ds(1, 15)], snd.at[2])
    arrived(m1.at[pl.ds(0, 14)], snd.at[4])
    arrived(fac.at[pl.ds(0, 3)], snd.at[5])
    arrived(m1.at[pl.ds(0, 14)], snd.at[6])
    arrived(m1.at[pl.ds(1, 15)], snd.at[7])
    arrived(yin.at[pl.ds(0, 2)], snd.at[8])
    arrived(rly, snd.at[9])
    early = pl.ds(0, G_GROUPS[DIRECT][0])
    arrived(g2.at[pl.ds(0, 2), early], snd.at[10])
    arrived(g2.at[0, early], snd.at[11])
    arrived(g2.at[pl.ds(0, 3), run((G_GROUPS[DIRECT][0], NZ))], snd.at[12])


def store_out(*refs):
    count = len(refs) // 2
    sem = refs[-1]
    copies = [pltpu.make_async_copy(refs[i], refs[count + i], sem.at[i]) for i in range(count)]
    for copy in copies:
        copy.start()
    for copy in copies:
        copy.wait()


def per_device(
    owners, inner_dense, anchor_dense, momentum_dense, inner_emb, anchor_emb, momentum_emb, basis
):
    mom = momentum_dense.reshape(NS, 512, LANES).transpose(1, 0, 2)
    mom = mom.reshape(NX, NZ, NC, NR, NS, LANES)
    dma = pltpu.SemaphoreType.DMA
    vmem = pltpu.VMEM
    vocab, width = anchor_emb.shape
    rank = basis.shape[1]
    results = pl.pallas_call(
        kernel,
        out_shape=(
            jax.ShapeDtypeStruct(anchor_dense.shape, F32),
            jax.ShapeDtypeStruct(mom.shape, F32),
            jax.ShapeDtypeStruct(anchor_emb.shape, F32),
            jax.ShapeDtypeStruct((rank, vocab), F32),
        ),
        in_specs=[pl.BlockSpec(memory_space=pltpu.HBM)] * 8,
        out_specs=[pl.BlockSpec(memory_space=pltpu.VMEM)] * 4,
        scratch_shapes=[
            vmem((1, 256), jnp.int32),
            vmem((256, LANES), F32),
            vmem((256, LANES), F32),
            vmem(mom.shape, F32),
            vmem((vocab, width), F32),
            vmem((vocab, width), F32),
            vmem((rank, vocab), F32),
            vmem((rank, width), F32),
            vmem((2, 128, LANES), F32),
            vmem((3, 256, LANES), F32),
            vmem((256, LANES), F32),
            vmem((512, 256), BF16),
            vmem((256, 512), BF16),
            vmem((NZ, NX, NC, NS, LANES), F32),
            vmem((NX, NC, NZ, NS, LANES), F32),
            vmem((NX, NC, NZ, NS, LANES), F32),
            vmem((NX, NC, NZ, NS, LANES), F32),
            vmem((NR, NZ, NX, NC, NS, LANES), F32),
            vmem((NR, rank, vocab), F32),
            dma((8,)),
            dma((6,)),
            dma((len(M_GROUPS),)),
            dma((len(M_GROUPS),)),
            dma((len(G_PLANE),)),
            dma((len(G_GROUPS),)),
            dma((len(G_GROUPS), 4)),
            dma((len(G_GROUPS), 2)),
            dma((6,)),
            dma((3,)),
            dma((13,)),
        ],
        compiler_params=pltpu.CompilerParams(
            collective_id=0, has_side_effects=True, vmem_limit_bytes=32 * 1024 * 1024
        ),
    )(*[
        pltpu.with_memory_space_constraint(v, pltpu.HBM)
        for v in (
            owners.reshape(1, 256), inner_dense[0], anchor_dense, mom, inner_emb[0], anchor_emb,
            momentum_emb.T, basis.T,
        )
    ])
    new_dense, new_mom, new_emb, new_memb = pl.pallas_call(
        store_out,
        out_shape=[jax.ShapeDtypeStruct(v.shape, v.dtype) for v in results],
        in_specs=[pl.BlockSpec(memory_space=pltpu.VMEM)] * 4,
        out_specs=[pl.BlockSpec(memory_space=pltpu.HBM)] * 4,
        scratch_shapes=[dma((4,))],
        compiler_params=pltpu.CompilerParams(vmem_limit_bytes=4 * 1024 * 1024),
    )(*results)
    new_mom = new_mom.reshape(512, NS, LANES).transpose(1, 0, 2).reshape(momentum_dense.shape)
    return new_dense, new_mom, new_emb, new_memb.T


def solution(mesh):
    placed = (
        P(),
        P("rep", None, "own"),
        P(None, "own"),
        P("own", None),
        P("rep", "own", None),
        P("own", None),
        P("own", None),
        P(),
    )
    return jax.shard_map(
        per_device,
        mesh=mesh,
        in_specs=placed,
        out_specs=(P(None, "own"), P("own", None), P("own", None), P("own", None)),
        check_vma=False,
    )
```

```python
import jax
import jax.numpy as jnp
from jax import lax
from jax.experimental import pallas as pl
from jax.experimental.pallas import tpu as pltpu
from jax.sharding import PartitionSpec as P

MESH = pl.DeviceIdType.MESH
RATE = 0.7
DECAY = 0.9
NX, NZ, NC, NR, NS = 4, 16, 2, 4, 4
LANES = 128
F32 = jnp.float32
BF16 = jnp.bfloat16
DISTANCE = (0, 1, 15, 2, 14, 3, 13, 4, 12, 5, 11, 6, 10, 7, 9, 8)
M_GROUPS = ((13, 16), (9, 13), (0, 9))
G_GROUPS = ((0, 5), (5, 9), (9, 13), (13, 15), (15, 16))
G_PLANE = ((0, 5), (5, 16))
DIRECT = 3


def split3(v):
    high = v.astype(BF16)
    rest = v - high.astype(F32)
    mid = rest.astype(BF16)
    low = (rest - mid.astype(F32)).astype(BF16)
    return high, mid, low


def select_rows(onehot, v):
    high, mid, low = split3(v)
    total = jnp.dot(onehot, low, preferred_element_type=F32)
    total = total + jnp.dot(onehot, mid, preferred_element_type=F32)
    return total + jnp.dot(onehot, high, preferred_element_type=F32)


def slot_of_distance(e):
    e = ((e + 8) & 15) - 8
    return jnp.minimum(jnp.where(e > 0, 2 * e - 1, -2 * e), 15)


def kernel(
    owners_hbm, inner_hbm, anchor_hbm, mom_hbm, iemb_hbm, aemb_hbm, memb_hbm, basis_hbm,
    nd_out, nm_out, ne_out, nme_out,
    owners, inq, anq, mom_v, ie, ae, memb, basis,
    rly, yin, gq, pack1, pick1, m1, m2, g0, g1, g2, fac,
    loc, rs_recv, mz_recv, mp_recv, gp_recv, gz_recv, gy_recv, gf_recv, nd_recv, f_recv, snd,
):
    own = lax.axis_index("own")
    rep = lax.axis_index("rep")
    c = lax.rem(own, NC)
    z = lax.rem(lax.div(own, NC), NZ)
    x = lax.div(own, NC * NZ)

    def position(px, pz, pc):
        return (px * NZ + pz) * NC + pc

    up = lax.rem(rep + 1, NR)
    down = lax.rem(rep + NR - 1, NR)
    across = lax.rem(rep + 2, NR)
    z_at = [lax.rem(z + d, NZ) for d in DISTANCE]
    z_peers = [{"rep": rep, "own": position(x, at, c)} for at in z_at]
    plane = []
    for dx in range(NX):
        for dc in range(NC):
            if dx or dc:
                px, pc = lax.rem(x + dx, NX), lax.rem(c + dc, NC)
                plane.append((px, pc, {"rep": rep, "own": position(px, z, pc)}))
    to_up = {"rep": up, "own": own}
    to_down = {"rep": down, "own": own}
    to_across = {"rep": across, "own": own}

    def local(src, dst, sem):
        copy = pltpu.make_async_copy(src, dst, sem)
        copy.start()

    def arrived(ref, sem):
        pltpu.make_async_copy(ref, ref, sem).wait()

    def send(src, dst, send_sem, recv_sem, peer):
        pltpu.make_async_remote_copy(
            src_ref=src, dst_ref=dst, send_sem=send_sem, recv_sem=recv_sem,
            device_id=peer, device_id_type=MESH,
        ).start()

    def columns(r):
        return pl.ds(pl.multiple_of(r * LANES, LANES), LANES)

    def run(ends):
        return pl.ds(ends[0], ends[1] - ends[0])

    half = (pl.ds(0, 128), pl.ds(128, 128))

    barrier = pltpu.get_barrier_semaphore()
    everyone = z_peers[1:] + [p[2] for p in plane] + [to_up, to_down, to_across]
    for peer in everyone:
        pl.semaphore_signal(barrier, inc=1, device_id=peer, device_id_type=MESH)

    local(owners_hbm, owners, loc.at[0])
    local(inner_hbm.at[:, columns(rep)], inq, loc.at[1])
    local(anchor_hbm.at[:, columns(rep)], anq, loc.at[2])
    local(mom_hbm.at[:, z, :, rep], m1.at[0], mz_recv.at[2])
    local(iemb_hbm, ie, loc.at[4])
    local(aemb_hbm, ae, loc.at[5])
    local(basis_hbm, basis, loc.at[6])
    local(memb_hbm, memb, loc.at[7])
    local(mom_hbm, mom_v, loc.at[3])

    pl.semaphore_wait(barrier, len(everyone))

    send(inner_hbm.at[:, columns(across)], yin.at[2], snd.at[1], rs_recv.at[4], to_across)
    send(inner_hbm.at[:, columns(up)], yin.at[0], snd.at[1], rs_recv.at[2], to_up)
    send(inner_hbm.at[:, columns(down)], yin.at[1], snd.at[1], rs_recv.at[3], to_down)

    for group, (low, high) in enumerate(M_GROUPS):
        for k in reversed(range(max(low, 1), high)):
            send(mom_hbm.at[:, z_at[k], :, rep], m1.at[k], snd.at[2], mz_recv.at[group], z_peers[k])

    arrived(owners, loc.at[0])
    names = owners[...]
    by_column = jnp.broadcast_to(names, (256, 256))
    by_row = by_column.T
    first = lax.broadcasted_iota(jnp.int32, (256, 256), 0)
    second = lax.broadcasted_iota(jnp.int32, (256, 256), 1)
    same = by_row == by_column
    slot_row = jnp.sum(jnp.where(same & (first < second), 1, 0), axis=0, keepdims=True)
    slot_column = jnp.sum(jnp.where(same & (second < first), 1, 0), axis=1, keepdims=True)

    def parts(p):
        return p >> 5, (p >> 1) & 15, p & 1

    ox, oz, oc = parts(names)
    pack_row = ((ox * NC + oc) * NZ + slot_of_distance(oz - z)) * NS + slot_row
    pack1[...] = jnp.where(
        lax.broadcasted_iota(jnp.int32, (512, 256), 0) == pack_row, 1.0, 0.0
    ).astype(BF16)
    ox, oz, oc = parts(by_row[:, 0:1])
    pick_column = ((ox * NC + oc) * NZ + slot_of_distance(z - oz)) * NS + slot_column
    pick1[...] = jnp.where(
        lax.broadcasted_iota(jnp.int32, (256, 512), 1) == pick_column, 1.0, 0.0
    ).astype(BF16)
    owned = jnp.sum(jnp.where(names == own, 1, 0), axis=1, keepdims=True)

    arrived(ie, loc.at[4])
    arrived(ae, loc.at[5])
    arrived(basis, loc.at[6])
    fac[rep] = lax.dot_general(
        basis[...], ae[...] - ie[...], (((1,), (1,)), ((), ())),
        precision=lax.Precision.HIGHEST, preferred_element_type=F32,
    )

    arrived(inq, loc.at[1])
    arrived(anq, loc.at[2])
    arrived(yin.at[0], rs_recv.at[2])
    arrived(yin.at[1], rs_recv.at[3])
    arrived(yin.at[2], rs_recv.at[4])
    anchor = anq[...]
    grad = (anchor - inq[...]) + (anchor - yin[0])
    grad = (grad + (anchor - yin[1]) + (anchor - yin[2])) * 0.25
    gq[...] = grad
    g0[...] = select_rows(pack1[...], grad).reshape(NX, NC, NZ, NS, LANES)
    for i, ends in enumerate(G_PLANE):
        for px, pc, peer in plane:
            send(g0.at[px, pc, run(ends)], g1.at[x, c, run(ends)], snd.at[4], gp_recv.at[i], peer)
        local(g0.at[x, c, run(ends)], g1.at[x, c, run(ends)], gp_recv.at[i])
    for i, peer in enumerate((to_up, to_down, to_across)):
        send(fac.at[rep], fac.at[rep], snd.at[5], f_recv.at[i], peer)

    def m_group(group):
        ends = M_GROUPS[group]
        arrived(m1.at[run(ends)], mz_recv.at[group])
        for px, pc, peer in plane:
            send(m1.at[run(ends), px, pc], m2.at[x, c, run(ends)], snd.at[6], mp_recv.at[group], peer)
        local(m1.at[run(ends), x, c], m2.at[x, c, run(ends)], mp_recv.at[group])

    m_group(0)
    m_group(1)
    m_group(2)
    group_of = [next(i for i, (a, b) in enumerate(G_GROUPS) if a <= k < b) for k in range(NZ)]
    for i, ends in enumerate(G_PLANE):
        arrived(g1.at[:, :, run(ends)], gp_recv.at[i])
        for k in range(max(ends[0], 1), ends[1]):
            send(g1.at[:, :, k], g2.at[rep, k], snd.at[7], gz_recv.at[group_of[k]], z_peers[k])
        if i == 0:
            local(g1.at[:, :, 0], g2.at[rep, 0], gz_recv.at[0])

    for group, ends in enumerate(M_GROUPS):
        arrived(m2.at[:, :, run(ends)], mp_recv.at[group])
    momentum = select_rows(pick1[...], m2[...].reshape(512, LANES))
    grad = gq[...]
    nd_out[:, columns(rep)] = anq[...] - RATE * (grad + DECAY * (DECAY * momentum + grad))

    def nd_part(r, h):
        return nd_out.at[half[h], columns(r)]

    send(nd_part(rep, 0), nd_part(rep, 0), snd.at[8], nd_recv.at[0], to_up)
    send(nd_part(rep, 1), nd_part(rep, 1), snd.at[8], nd_recv.at[3], to_down)
    send(nd_part(rep, 1), nd_part(rep, 1), snd.at[8], nd_recv.at[1], to_up)
    send(nd_part(rep, 0), nd_part(rep, 0), snd.at[8], nd_recv.at[2], to_down)

    def g_part(r, group, h):
        return g2.at[r, run(G_GROUPS[group]), pl.ds(2 * h, 2)]

    def g_share(group):
        arrived(g2.at[rep, run(G_GROUPS[group])], gz_recv.at[group])
        if group >= DIRECT:
            whole = g2.at[rep, run(G_GROUPS[group])]
            for sem, peer in ((2, to_across), (0, to_up), (1, to_down)):
                send(whole, whole, snd.at[12], gy_recv.at[group, sem], peer)
            return
        for h, sem, peer in ((0, 0, to_up), (1, 3, to_down), (1, 1, to_up), (0, 2, to_down)):
            part = g_part(rep, group, h)
            send(part, part, snd.at[10], gy_recv.at[group, sem], peer)

    def g_relay(group):
        if group >= DIRECT:
            return
        arrived(g_part(down, group, 0), gy_recv.at[group, 0])
        send(g_part(down, group, 0), g_part(down, group, 0), snd.at[11], gf_recv.at[group, 0], to_up)
        arrived(g_part(up, group, 1), gy_recv.at[group, 3])
        send(g_part(up, group, 1), g_part(up, group, 1), snd.at[11], gf_recv.at[group, 1], to_down)

    g_share(0)

    arrived(memb, loc.at[7])
    arrived(fac.at[down], f_recv.at[0])
    arrived(fac.at[up], f_recv.at[1])
    arrived(fac.at[across], f_recv.at[2])
    mean_factor = ((fac[0] + fac[1]) + (fac[2] + fac[3])) * 0.25
    new_memb = DECAY * memb[...] + mean_factor
    nme_out[...] = new_memb
    emb_update = mean_factor + DECAY * new_memb
    ne_out[...] = ae[...] - RATE * lax.dot_general(
        emb_update, basis[...], (((0,), (0,)), ((), ())),
        precision=lax.Precision.HIGHEST, preferred_element_type=F32,
    )

    arrived(nd_part(down, 0), nd_recv.at[0])
    send(nd_part(down, 0), nd_part(down, 0), snd.at[9], nd_recv.at[4], to_up)
    arrived(nd_part(up, 1), nd_recv.at[3])
    send(nd_part(up, 1), nd_part(up, 1), snd.at[9], nd_recv.at[5], to_down)
    g_relay(0)
    for group in range(1, len(G_GROUPS)):
        g_share(group)
        if group > 1:
            g_relay(group - 1)
    g_relay(len(G_GROUPS) - 1)

    arrived(nd_part(down, 1), nd_recv.at[1])
    arrived(nd_part(up, 0), nd_recv.at[2])
    arrived(nd_part(across, 0), nd_recv.at[4])
    arrived(nd_part(across, 1), nd_recv.at[5])
    arrived(mom_v, loc.at[3])
    live = lax.broadcasted_iota(jnp.int32, (NS, LANES), 0) < owned

    def finish(k, carry):
        steps = lax.div(k + 1, 2)
        at = lax.rem(z + NZ + (1 - 2 * lax.rem(k, 2)) * steps, NZ)
        for px in range(NX):
            for pc in range(NC):
                for r in range(NR):
                    value = DECAY * mom_v[px, at, pc, r] + g2[r, k, px, pc]
                    nm_out[px, at, pc, r] = jnp.where(live, value, 0.0)
        return carry

    for group, ends in enumerate(G_GROUPS):
        if group >= DIRECT:
            for sem, r in enumerate((down, up, across)):
                arrived(g2.at[r, run(ends)], gy_recv.at[group, sem])
        else:
            arrived(g_part(down, group, 1), gy_recv.at[group, 1])
            arrived(g_part(up, group, 0), gy_recv.at[group, 2])
            arrived(g_part(across, group, 0), gf_recv.at[group, 0])
            arrived(g_part(across, group, 1), gf_recv.at[group, 1])
        lax.fori_loop(ends[0], ends[1], finish, 0)

    arrived(yin, snd.at[1])
    arrived(m1.at[pl.ds(1, 15)], snd.at[2])
    arrived(m1.at[pl.ds(0, 14)], snd.at[4])
    arrived(fac.at[pl.ds(0, 3)], snd.at[5])
    arrived(m1.at[pl.ds(0, 14)], snd.at[6])
    arrived(m1.at[pl.ds(1, 15)], snd.at[7])
    arrived(yin.at[pl.ds(0, 2)], snd.at[8])
    arrived(rly, snd.at[9])
    early = pl.ds(0, G_GROUPS[DIRECT][0])
    arrived(g2.at[pl.ds(0, 2), early], snd.at[10])
    arrived(g2.at[0, early], snd.at[11])
    arrived(g2.at[pl.ds(0, 3), run((G_GROUPS[DIRECT][0], NZ))], snd.at[12])


def store_out(*refs):
    count = len(refs) // 2
    sem = refs[-1]
    copies = [pltpu.make_async_copy(refs[i], refs[count + i], sem.at[i]) for i in range(count)]
    for copy in copies:
        copy.start()
    for copy in copies:
        copy.wait()


def per_device(
    owners, inner_dense, anchor_dense, momentum_dense, inner_emb, anchor_emb, momentum_emb, basis
):
    mom = momentum_dense.reshape(NS, 512, LANES).transpose(1, 0, 2)
    mom = mom.reshape(NX, NZ, NC, NR, NS, LANES)
    dma = pltpu.SemaphoreType.DMA
    vmem = pltpu.VMEM
    vocab, width = anchor_emb.shape
    rank = basis.shape[1]
    results = pl.pallas_call(
        kernel,
        out_shape=(
            jax.ShapeDtypeStruct(anchor_dense.shape, F32),
            jax.ShapeDtypeStruct(mom.shape, F32),
            jax.ShapeDtypeStruct(anchor_emb.shape, F32),
            jax.ShapeDtypeStruct((rank, vocab), F32),
        ),
        in_specs=[pl.BlockSpec(memory_space=pltpu.HBM)] * 8,
        out_specs=[pl.BlockSpec(memory_space=pltpu.VMEM)] * 4,
        scratch_shapes=[
            vmem((1, 256), jnp.int32),
            vmem((256, LANES), F32),
            vmem((256, LANES), F32),
            vmem(mom.shape, F32),
            vmem((vocab, width), F32),
            vmem((vocab, width), F32),
            vmem((rank, vocab), F32),
            vmem((rank, width), F32),
            vmem((2, 128, LANES), F32),
            vmem((3, 256, LANES), F32),
            vmem((256, LANES), F32),
            vmem((512, 256), BF16),
            vmem((256, 512), BF16),
            vmem((NZ, NX, NC, NS, LANES), F32),
            vmem((NX, NC, NZ, NS, LANES), F32),
            vmem((NX, NC, NZ, NS, LANES), F32),
            vmem((NX, NC, NZ, NS, LANES), F32),
            vmem((NR, NZ, NX, NC, NS, LANES), F32),
            vmem((NR, rank, vocab), F32),
            dma((8,)),
            dma((6,)),
            dma((len(M_GROUPS),)),
            dma((len(M_GROUPS),)),
            dma((len(G_PLANE),)),
            dma((len(G_GROUPS),)),
            dma((len(G_GROUPS), 4)),
            dma((len(G_GROUPS), 2)),
            dma((6,)),
            dma((3,)),
            dma((13,)),
        ],
        compiler_params=pltpu.CompilerParams(
            collective_id=0, has_side_effects=True, vmem_limit_bytes=32 * 1024 * 1024
        ),
    )(*[
        pltpu.with_memory_space_constraint(v, pltpu.HBM)
        for v in (
            owners.reshape(1, 256), inner_dense[0], anchor_dense, mom, inner_emb[0], anchor_emb,
            momentum_emb.T, basis.T,
        )
    ])
    new_dense, new_mom, new_emb, new_memb = pl.pallas_call(
        store_out,
        out_shape=[jax.ShapeDtypeStruct(v.shape, v.dtype) for v in results],
        in_specs=[pl.BlockSpec(memory_space=pltpu.VMEM)] * 4,
        out_specs=[pl.BlockSpec(memory_space=pltpu.HBM)] * 4,
        scratch_shapes=[dma((4,))],
        compiler_params=pltpu.CompilerParams(vmem_limit_bytes=4 * 1024 * 1024),
    )(*results)
    new_mom = new_mom.reshape(512, NS, LANES).transpose(1, 0, 2).reshape(momentum_dense.shape)
    return new_dense, new_mom, new_emb, new_memb.T


def solution(mesh):
    placed = (
        P(),
        P("rep", None, "own"),
        P(None, "own"),
        P("own", None),
        P("rep", "own", None),
        P("own", None),
        P("own", None),
        P(),
    )
    return jax.shard_map(
        per_device,
        mesh=mesh,
        in_specs=placed,
        out_specs=(P(None, "own"), P("own", None), P("own", None), P("own", None)),
        check_vma=False,
    )
```
